32 devices in a mesh: dp: 8 (over y, x, core), context: 4 (over z).
Axes of the slice: x: 2, y: 2, z: 4, core: 2. Of those that a mesh axis runs over, the one named last changes fastest.
Arguments:
- image_tokens: bfloat16 [8, 448, 3072], P('dp', 'context'), may hold values from -6 to 6
- text_tokens: bfloat16 [8, 64, 3072], P('dp', 'context'), may hold values from -6 to 6
- image_mod: bfloat16 [8, 3, 3072], P('dp'), may hold values from -4 to 4
- text_mod: bfloat16 [8, 3, 3072], P('dp'), may hold values from -4 to 4
- image_qkv_weight: bfloat16 [3072, 3, 16, 128], P('dp', None, 'context'), may hold values from -0.109375 to 0.109375
- text_qkv_weight: bfloat16 [3072, 3, 16, 128], P('dp', None, 'context'), may hold values from -0.109375 to 0.109375
- image_out_weight: bfloat16 [3072, 16, 128], P('dp', 'context'), may hold values from -1 to 1
- text_out_weight: bfloat16 [3072, 16, 128], P('dp', 'context'), may hold values from -1 to 1
- image_slope: bfloat16 [8, 448, 3072], P('dp', 'context'), may hold values from -0.119628906 to 0.119628906
- text_slope: bfloat16 [8, 64, 3072], P('dp', 'context'), may hold values from -0.119628906 to 0.119628906
Outputs:
- image_update: bfloat16 [8, 448, 3072], P('dp', 'context')
- text_update: bfloat16 [8, 64, 3072], P('dp', 'context')
- image_qkv_grad: float32 [3072, 3, 16, 128], P('dp', None, 'context')
- text_qkv_grad: float32 [3072, 3, 16, 128], P('dp', None, 'context')
- image_out_grad: float32 [3072, 16, 128], P('dp', 'context')
- text_out_grad: float32 [3072, 16, 128], P('dp', 'context')
- image_mod_grad: float32 [8, 3, 3072], P('dp')
- text_mod_grad: float32 [8, 3, 3072], P('dp')
The draws below stay inside these ranges and needn't reach their ends.
All inputs are finite; a program needn't handle non-finite values.
Results may differ from the reference program's by a relative error of at most 0.015.
Values may be sent and summed in bfloat16 or wider, within the bound.
No kernel may reach another device: no remote copies, remote signals or barrier semaphores. Data moves between devices by JAX's collectives and lax.ppermute only.
A program may use at most 128 MiB of HBM per device.

```python
import jax
import jax.numpy as jnp
from jax import lax

D = 3072
H = 16
HD = 128
IMG = 448
TXT = 64
SEQ = 512
IMAGES = 8
N_CONTEXT = 4


def block_levels(own_key, dims, split, least, high):
    gain = 1.0
    for axis_at, blocks in split:
        draws = jax.random.uniform(jax.random.fold_in(jax.random.fold_in(own_key, 6), axis_at), (blocks,), jnp.float32, least / len(split), high / len(split))
        gain = gain * jnp.repeat(jnp.exp(draws), dims[axis_at] // blocks).reshape((-1,) + (1,) * (len(dims) - 1 - axis_at))
    return gain


def bell_draw(rng, shape, width, reach, cuts=(), dtype=jnp.bfloat16):
    level = block_levels(rng, shape, cuts, -0.22, 0.18) if cuts else 1.0
    values = jax.random.normal(rng, shape, jnp.float32) * width * level
    return jnp.minimum(jnp.maximum(values, -reach), reach).astype(dtype)


def setup_inputs(seed: int = 0) -> dict:
    key_list = jax.random.split(jax.random.key(seed), 11)
    return {
        "image_tokens": bell_draw(key_list[0], (IMAGES, IMG, D), 1.0, 6.0, ((0, 8), (1, 4))),
        "text_tokens": bell_draw(key_list[1], (IMAGES, TXT, D), 1.0, 6.0, ((0, 8), (1, 4))),
        "image_mod": bell_draw(key_list[2], (IMAGES, 3, D), 0.8, 4.0, ((0, 8),)),
        "text_mod": bell_draw(key_list[3], (IMAGES, 3, D), 0.8, 4.0, ((0, 8),)),
        "image_qkv_weight": bell_draw(key_list[4], (D, 3, H, HD), D ** -0.5, 0.109375, ((0, 8), (2, 4))),
        "text_qkv_weight": bell_draw(key_list[5], (D, 3, H, HD), D ** -0.5, 0.109375, ((0, 8), (2, 4))),
        "image_out_weight": bell_draw(key_list[6], (D, H, HD), (HD // 4) ** -0.5, 1.0, ((0, 8), (1, 4))),
        "text_out_weight": bell_draw(key_list[7], (D, H, HD), (HD // 4) ** -0.5, 1.0, ((0, 8), (1, 4))),
        "image_slope": bell_draw(key_list[8], (IMAGES, IMG, D), 0.02, 0.119628906, ((0, 8), (1, 4))),
        "text_slope": bell_draw(key_list[9], (IMAGES, TXT, D), 0.02, 0.119628906, ((0, 8), (1, 4))),
    }


norm_eps = 1e-06

def layer_normal(values):
    average = lax.optimization_barrier(jnp.mean(values, axis=-1, keepdims=True))
    centred = values - average
    return centred * lax.rsqrt(lax.optimization_barrier(jnp.mean(centred * centred, axis=-1, keepdims=True)) + norm_eps)

def rms_normal(values):
    factor = lax.rsqrt(lax.optimization_barrier(jnp.mean(values * values, axis=-1, keepdims=True)) + norm_eps)
    return (values * factor, factor)

def rms_back(normed, factor, slopes):
    return factor * (slopes - normed * lax.optimization_barrier(jnp.mean(slopes * normed, axis=-1, keepdims=True)))

def to_bf(values):
    return lax.optimization_barrier(values.astype(jnp.bfloat16))

def modulate(tokens, modulation):
    normal = layer_normal(tokens.astype(jnp.float32))
    factors = modulation.astype(jnp.float32)
    return (normal, ((1.0 + factors[1]) * normal + factors[0]).astype(jnp.bfloat16))

def grouped_sum(attended_rows, out_flat):
    row_total = attended_rows.shape[0]
    group_width = H // N_CONTEXT * HD
    left_side = attended_rows.astype(jnp.float32).reshape(row_total, N_CONTEXT, group_width)
    right_side = out_flat.astype(jnp.float32).reshape(D, N_CONTEXT, group_width)
    partial_value = jnp.einsum('tcx,dcx->ctd', left_side, right_side)
    return lax.optimization_barrier(jnp.sum(to_bf(partial_value).astype(jnp.float32), axis=0))

def reference(image_tokens, text_tokens, image_mod, text_mod, image_qkv_weight, text_qkv_weight, image_out_weight, text_out_weight, image_slope, text_slope):
    triple = 3 * H * HD
    inner_width = H * HD
    score_scale = HD ** (-0.5)
    wq_image = image_qkv_weight.reshape(D, triple)
    wq_text = text_qkv_weight.reshape(D, triple)
    wo_image = image_out_weight.reshape(D, inner_width)
    wo_text = text_out_weight.reshape(D, inner_width)

    def one_image(totals, inputs):
        tokens_image, tokens_text, mod_image, mod_text, slope_image, slope_text = inputs
        normal_image, input_image = modulate(tokens_image, mod_image)
        normal_text, input_text = modulate(tokens_text, mod_text)
        projected = jnp.concatenate([jnp.dot(input_text, wq_text, preferred_element_type=jnp.float32), jnp.dot(input_image, wq_image, preferred_element_type=jnp.float32)], axis=0).reshape(SEQ, 3, H, HD)
        query_normal, query_factor = rms_normal(projected[:, 0])
        key_normal, key_factor = rms_normal(projected[:, 1])
        query_b = to_bf(query_normal).astype(jnp.float32)
        key_b = to_bf(key_normal).astype(jnp.float32)
        value_b = to_bf(projected[:, 2]).astype(jnp.float32)
        scores = jnp.einsum('ihe,jhe->hij', query_b, key_b) * score_scale
        raised = jnp.exp(scores)
        attn_probs = raised / lax.optimization_barrier(jnp.sum(raised, axis=-1, keepdims=True))
        probs_b = to_bf(attn_probs)
        probs_f = probs_b.astype(jnp.float32)
        attended = to_bf(jnp.einsum('hij,jhe->ihe', probs_f, value_b)).reshape(SEQ, inner_width)
        att_text = attended[:TXT]
        att_image = attended[TXT:]
        mixed_text = grouped_sum(att_text, wo_text)
        mixed_image = grouped_sum(att_image, wo_image)
        factors_image = mod_image.astype(jnp.float32)
        factors_text = mod_text.astype(jnp.float32)
        update_image = (factors_image[2] * mixed_image).astype(jnp.bfloat16)
        update_text = (factors_text[2] * mixed_text).astype(jnp.bfloat16)
        slope_image_f = slope_image.astype(jnp.float32)
        slope_text_f = slope_text.astype(jnp.float32)
        gated_image = (factors_image[2] * slope_image_f).astype(jnp.bfloat16)
        gated_text = (factors_text[2] * slope_text_f).astype(jnp.bfloat16)
        back_att = to_bf(jnp.concatenate([jnp.dot(gated_text, wo_text, preferred_element_type=jnp.float32), jnp.dot(gated_image, wo_image, preferred_element_type=jnp.float32)], axis=0))
        back_att_f = back_att.astype(jnp.float32).reshape(SEQ, H, HD)
        back_probs = jnp.einsum('ihe,jhe->hij', back_att_f, value_b)
        back_value = jnp.einsum('hij,ihe->jhe', probs_f, back_att_f)
        back_scores = to_bf(attn_probs * (back_probs - lax.optimization_barrier(jnp.sum(attn_probs * back_probs, axis=-1, keepdims=True))) * score_scale).astype(jnp.float32)
        back_query = jnp.einsum('hij,jhe->ihe', back_scores, key_b)
        back_key = jnp.einsum('hij,ihe->jhe', back_scores, query_b)
        back_qkv = jnp.stack([rms_back(query_normal, query_factor, back_query), rms_back(key_normal, key_factor, back_key), back_value], axis=1).reshape(SEQ, triple).astype(jnp.bfloat16)
        back_text = back_qkv[:TXT]
        back_image = back_qkv[TXT:]
        grad_q_image = to_bf(jnp.dot(input_image.T, back_image, preferred_element_type=jnp.float32)).astype(jnp.float32)
        grad_q_text = to_bf(jnp.dot(input_text.T, back_text, preferred_element_type=jnp.float32)).astype(jnp.float32)
        grad_o_image = to_bf(jnp.dot(gated_image.T, att_image, preferred_element_type=jnp.float32)).astype(jnp.float32)
        grad_o_text = to_bf(jnp.dot(gated_text.T, att_text, preferred_element_type=jnp.float32)).astype(jnp.float32)
        spread_image = jnp.dot(back_image, wq_image.T, preferred_element_type=jnp.float32)
        spread_text = jnp.dot(back_text, wq_text.T, preferred_element_type=jnp.float32)
        modgrad_image = jnp.stack([lax.optimization_barrier(jnp.sum(spread_image, axis=0)), lax.optimization_barrier(jnp.sum(spread_image * normal_image, axis=0)), lax.optimization_barrier(jnp.sum(slope_image_f * mixed_image, axis=0))])
        modgrad_text = jnp.stack([lax.optimization_barrier(jnp.sum(spread_text, axis=0)), lax.optimization_barrier(jnp.sum(spread_text * normal_text, axis=0)), lax.optimization_barrier(jnp.sum(slope_text_f * mixed_text, axis=0))])
        totals = (totals[0] + grad_q_image, totals[1] + grad_q_text, totals[2] + grad_o_image, totals[3] + grad_o_text)
        return (totals, (update_image, update_text, modgrad_image, modgrad_text))
    start_totals = (jnp.zeros((D, triple), jnp.float32), jnp.zeros((D, triple), jnp.float32), jnp.zeros((D, inner_width), jnp.float32), jnp.zeros((D, inner_width), jnp.float32))
    totals, stacked = lax.scan(one_image, start_totals, (image_tokens, text_tokens, image_mod, text_mod, image_slope, text_slope))
    return (stacked[0], stacked[1], totals[0].reshape(D, 3, H, HD), totals[1].reshape(D, 3, H, HD), totals[2].reshape(D, H, HD), totals[3].reshape(D, H, HD), stacked[2], stacked[3])
```

```python
import functools

import jax
import jax.numpy as jnp
from jax import lax
from jax.experimental import pallas as pl
from jax.experimental.pallas import tpu as pltpu
from jax.sharding import PartitionSpec as P


norm_eps = 1e-06
bf16 = jnp.bfloat16
f32 = jnp.float32


def layer_normal(values):
    average = jnp.mean(values, axis=-1, keepdims=True)
    centred = values - average
    return centred * lax.rsqrt(jnp.mean(centred * centred, axis=-1, keepdims=True) + norm_eps)


def rms_factor(values):
    return lax.rsqrt(jnp.mean(values * values, axis=-1, keepdims=True) + norm_eps)


def dot(left, right, left_dim=1, right_dim=0):
    return lax.dot_general(
        left, right, (((left_dim,), (right_dim,)), ((), ())), preferred_element_type=f32
    )


def dp_swap(value, mask):
    count = lax.axis_size("dp")
    return lax.ppermute(value, "dp", [(at, at ^ mask) for at in range(count)])


def context_shift(value):
    count = lax.axis_size("context")
    return lax.ppermute(value, "context", [(at, (at + 1) % count) for at in range(count)])


def context_swap(value, mask):
    count = lax.axis_size("context")
    return lax.ppermute(value, "context", [(at, at ^ mask) for at in range(count)])


def mask_order():
    count = lax.axis_size("dp")
    return [2 * (p % (count // 2)) + p // (count // 2) for p in range(count)]


def chip_bits():
    count, bit, found = lax.axis_size("dp"), 2, []
    while bit < count:
        found.append(bit)
        bit *= 2
    return found


def gather_chips(value, bits):
    pieces = {0: value}
    for bit in bits:
        for mask in list(pieces):
            pieces[mask | bit] = dp_swap(pieces[mask], bit)
    return pieces


def gather_cores(pieces):
    both = dict(pieces)
    for mask, value in pieces.items():
        both[mask | 1] = dp_swap(value, 1)
    return [both[mask] for mask in mask_order()]


def gather_small(value):
    pieces = {mask: dp_swap(value, mask) for mask in range(2, lax.axis_size("dp"), 2)}
    pieces[0] = value
    evens = jnp.stack([pieces[mask] for mask in sorted(pieces)])
    return jnp.concatenate([evens, dp_swap(evens, 1)], axis=0)


def exchange(blocks):
    order = mask_order()
    return [blocks[p] if mask == 0 else dp_swap(blocks[p], mask) for p, mask in enumerate(order)]


def reduce_chips(blocks, bits):
    for bit in bits:
        kept = [mask for mask in blocks if not mask & bit]
        blocks = {
            mask: blocks[mask] + dp_swap(blocks[mask | bit].astype(bf16), bit).astype(f32)
            for mask in kept
        }
    return blocks[0]


def reduce_dp(odd, even_rows, shard_rows):
    summed = even_rows + dp_swap(odd, 1).astype(f32)
    bits = chip_bits()
    half = summed.shape[1] // 2
    parts = []
    for part, order in enumerate((bits, bits[::-1])):
        blocks = {
            2 * at: summed[at * shard_rows : (at + 1) * shard_rows, part * half : (part + 1) * half]
            for at in range(lax.axis_size("dp") // 2)
        }
        parts.append(reduce_chips(blocks, order))
    return jnp.concatenate(parts, axis=1)


def relative_block(place, me_ref, count):
    mask = 2 * lax.rem(place, count // 2) + lax.div(place, count // 2)
    return lax.bitwise_xor(me_ref[0], mask)


def place_of(block, me_ref, count):
    mask = lax.bitwise_xor(me_ref[0], block)
    return lax.rem(mask, 2) * (count // 2) + lax.div(mask, 2)


def enter_kernel(me, tok, slope, text, text_slope, mods_i, mods_t, tok_o, gated_o, text_o, mi_o, mt_o):
    gate_i = mods_i[2:3, :].astype(f32)
    gate_t = mods_t[2:3, :].astype(f32)
    tok_o[...] = tok[...]
    gated_o[...] = (gate_i * slope[...].astype(f32)).astype(bf16)
    width = text.shape[1]
    text_o[0, :, :width] = text[...]
    text_o[0, :, width:] = (gate_t * text_slope[...].astype(f32)).astype(bf16)
    mi_o[...] = mods_i[...].astype(f32)
    mt_o[...] = mods_t[...].astype(f32)


def take_blocks(values, places):
    count = lax.axis_size("dp")
    blocks = values.reshape(values.shape[0], count, values.shape[1] // count)
    return jnp.take(blocks, places, axis=1).reshape(values.shape)


def enter(me, tok, slope, text, text_slope, mods_i, mods_t):
    count = lax.axis_size("dp")
    width = tok.shape[1] // count
    if width % 128:
        places = me ^ jnp.array(mask_order(), jnp.int32)
        arrays = (tok, slope, text, text_slope, mods_i.astype(f32), mods_t.astype(f32))
        tok, slope, text, text_slope, mods_i, mods_t = (take_blocks(a, places) for a in arrays)
        gated = (mods_i[2] * slope.astype(f32)).astype(bf16)
        text_gated = (mods_t[2] * text_slope.astype(f32)).astype(bf16)
        both = [a.reshape(-1, count, width).swapaxes(0, 1) for a in (text, text_gated)]
        return tok, gated, jnp.concatenate(both, axis=2), mods_i, mods_t

    def spec(rows):
        return pl.BlockSpec((rows, width), lambda p, me: (0, relative_block(p, me, count)))

    def out(rows):
        return pl.BlockSpec((rows, width), lambda p, me: (0, p))

    arrays = (tok, slope, text, text_slope, mods_i, mods_t)
    rows_t = text.shape[0]
    return pl.pallas_call(
        enter_kernel,
        grid_spec=pltpu.PrefetchScalarGridSpec(
            num_scalar_prefetch=1,
            grid=(count,),
            in_specs=[spec(a.shape[0]) for a in arrays],
            out_specs=[
                out(tok.shape[0]),
                out(tok.shape[0]),
                pl.BlockSpec((1, rows_t, 2 * width), lambda p, me: (p, 0, 0)),
                out(3),
                out(3),
            ],
        ),
        out_shape=[
            jax.ShapeDtypeStruct(tok.shape, bf16),
            jax.ShapeDtypeStruct(tok.shape, bf16),
            jax.ShapeDtypeStruct((count, rows_t, 2 * width), bf16),
            jax.ShapeDtypeStruct(mods_i.shape, f32),
            jax.ShapeDtypeStruct(mods_t.shape, f32),
        ],
        name="enter",
    )(me, *arrays)


def leave_kernel(me, up_i, up_t, grad_i, grad_t, up_i_o, up_t_o, grad_i_o, grad_t_o):
    up_i_o[...] = up_i[...]
    up_t_o[...] = up_t[...]
    grad_i_o[...] = grad_i[...]
    grad_t_o[...] = grad_t[...]


def leave(me, *arrays):
    count = lax.axis_size("dp")
    width = arrays[0].shape[1] // count
    if width % 128:
        masks = me ^ jnp.arange(count, dtype=jnp.int32)
        return [take_blocks(a, masks % 2 * (count // 2) + masks // 2) for a in arrays]
    return pl.pallas_call(
        leave_kernel,
        grid_spec=pltpu.PrefetchScalarGridSpec(
            num_scalar_prefetch=1,
            grid=(count,),
            in_specs=[
                pl.BlockSpec((a.shape[0], width), lambda d, me: (0, place_of(d, me, count)))
                for a in arrays
            ],
            out_specs=[pl.BlockSpec((a.shape[0], width), lambda d, me: (0, d)) for a in arrays],
        ),
        out_shape=[jax.ShapeDtypeStruct(a.shape, a.dtype) for a in arrays],
        name="leave",
    )(me, *arrays)


def forward_kernel(scale, qi, ki, vi, qt, kt, vt, att_i, att_t):
    rows = qi.shape[0]
    query = jnp.concatenate([qi[...], qt[...]], axis=0)
    key = jnp.concatenate([ki[...], kt[...]], axis=0)
    value = jnp.concatenate([vi[...], vt[...]], axis=0).astype(bf16)
    query = (query * rms_factor(query)).astype(bf16)
    key = (key * rms_factor(key)).astype(bf16)
    raised = jnp.exp(dot(query, key, 1, 1) * scale)
    probs = raised / jnp.sum(raised, axis=-1, keepdims=True)
    attended = dot(probs.astype(bf16), value).astype(bf16)
    att_i[...] = attended[:rows]
    att_t[...] = attended[rows:]


def attention_forward(qk, v, text, heads):
    size = v.shape[1] // heads
    rows, rows_t = v.shape[0], text.shape[0]

    def spec(n, at):
        return pl.BlockSpec((n, size), lambda h: (0, at * heads + h))

    return pl.pallas_call(
        functools.partial(forward_kernel, size ** (-0.5)),
        grid=(heads,),
        in_specs=[
            spec(rows, 0),
            spec(rows, 1),
            spec(rows, 0),
            spec(rows_t, 0),
            spec(rows_t, 1),
            spec(rows_t, 2),
        ],
        out_specs=[spec(rows, 0), spec(rows_t, 0)],
        out_shape=[
            jax.ShapeDtypeStruct((rows, heads * size), bf16),
            jax.ShapeDtypeStruct((rows_t, heads * size), bf16),
        ],
        name="attention_forward",
    )(qk, qk, v, text, text, text)


def backward_kernel(scale, blocks, *refs):
    qi, ki, vi, qt, kt, vt, bt = refs[:7]
    back_refs = refs[7 : 7 + blocks]
    bq_i, bk_i, bv_i, b_t = refs[7 + blocks :]
    rows = qi.shape[0]
    query = jnp.concatenate([qi[...], qt[...]], axis=0)
    key = jnp.concatenate([ki[...], kt[...]], axis=0)
    value = jnp.concatenate([vi[...], vt[...]], axis=0).astype(bf16)
    back = jnp.concatenate([r[...] for r in back_refs] + [bt[...].astype(bf16)], axis=0)
    query_factor = rms_factor(query)
    key_factor = rms_factor(key)
    query_normal = query * query_factor
    key_normal = key * key_factor
    query_b = query_normal.astype(bf16)
    key_b = key_normal.astype(bf16)
    raised = jnp.exp(dot(key_b, query_b, 1, 1) * scale)
    probs = raised / jnp.sum(raised, axis=0, keepdims=True)
    back_probs = dot(value, back, 1, 1)
    inner = jnp.sum(probs * back_probs, axis=0, keepdims=True)
    back_scores = (probs * (back_probs - inner) * scale).astype(bf16)
    back_value = dot(probs.astype(bf16), back)
    back_key = dot(back_scores, query_b)
    back_query = dot(back_scores, key_b, 0, 0)
    back_query = query_factor * (
        back_query - query_normal * jnp.mean(back_query * query_normal, axis=-1, keepdims=True)
    )
    back_key = key_factor * (
        back_key - key_normal * jnp.mean(back_key * key_normal, axis=-1, keepdims=True)
    )
    for at, (out, values) in enumerate(((bq_i, back_query), (bk_i, back_key), (bv_i, back_value))):
        rounded = values.astype(bf16)
        out[...] = rounded[:rows]
        b_t[at] = rounded[rows:]


def attention_backward(qk, v, text, back_blocks, heads):
    size = v.shape[1] // heads
    rows, rows_t = v.shape[0], text.shape[0]

    def spec(n, at):
        return pl.BlockSpec((n, size), lambda h: (0, at * heads + h))

    image = jax.ShapeDtypeStruct((rows, heads * size), bf16)
    return pl.pallas_call(
        functools.partial(backward_kernel, size ** (-0.5), len(back_blocks)),
        grid=(heads,),
        in_specs=[
            spec(rows, 0),
            spec(rows, 1),
            spec(rows, 0),
            spec(rows_t, 0),
            spec(rows_t, 1),
            spec(rows_t, 2),
            spec(rows_t, 3),
        ]
        + [spec(b.shape[0], 0) for b in back_blocks],
        out_specs=[spec(rows, 0)] * 3 + [pl.BlockSpec((3, rows_t, size), lambda h: (0, 0, h))],
        out_shape=[image] * 3 + [jax.ShapeDtypeStruct((3, rows_t, heads * size), bf16)],
        name="attention_backward",
    )(qk, qk, v, text, text, text, text, *back_blocks)


def body(
    image_tokens,
    text_tokens,
    image_mod,
    text_mod,
    image_qkv_weight,
    text_qkv_weight,
    image_out_weight,
    text_out_weight,
    image_slope,
    text_slope,
):
    count = lax.axis_size("dp")
    groups = lax.axis_size("context")
    me = lax.axis_index("dp").astype(jnp.int32).reshape(1)
    own_image = image_tokens.shape[1]
    own_text = text_tokens.shape[1]
    width = image_tokens.shape[2]
    shard_rows, _, heads, size = image_qkv_weight.shape
    inner = heads * size
    triple = 3 * inner
    bits = chip_bits()
    order = mask_order()

    text_mods = text_mod[0].astype(f32)
    text_normal = layer_normal(text_tokens[0].astype(f32))
    text_input = ((1.0 + text_mods[1]) * text_normal + text_mods[0]).astype(bf16)
    tokens0, gated0, text_blocks, mods_i, mods_t = enter(
        me, image_tokens[0], image_slope[0], text_input, text_slope[0], image_mod[0], text_mod[0]
    )

    text_recv = jnp.stack(exchange([text_blocks[p] for p in range(count)]))
    text_ring = [text_recv]
    for _ in range(groups - 1):
        text_ring.append(context_shift(text_ring[-1]))

    token_ring = [tokens0]
    for _ in range(groups - 1):
        token_ring.append(context_shift(token_ring[-1]))
    gated_start, _ = lax.optimization_barrier((gated0, token_ring[groups - 2]))
    gated_ring = [gated_start]
    for _ in range(groups - 1):
        gated_ring.append(context_shift(gated_ring[-1]))

    flat_q = image_qkv_weight.reshape(shard_rows, triple)
    flat_o = image_out_weight.reshape(shard_rows, inner)
    part_a = flat_q[:, : 2 * inner]
    part_b = jnp.concatenate([flat_q[:, 2 * inner :], flat_o], axis=1)
    pieces_b = gather_cores(gather_chips(part_b, bits[::-1]))
    pieces_a = gather_cores(gather_chips(part_a, bits))
    w_qk = jnp.concatenate(pieces_a, axis=0)
    w_v = jnp.concatenate([piece[:, :inner] for piece in pieces_b], axis=0)
    w_o = jnp.concatenate([piece[:, inner:] for piece in pieces_b], axis=0)

    wq_text = text_qkv_weight.reshape(shard_rows, triple)
    wo_text = text_out_weight.reshape(shard_rows, inner)
    text_cols = jnp.stack(text_ring, axis=1).reshape(count * groups * own_text, 2 * shard_rows)
    input_cols = text_cols[:, :shard_rows]
    gated_cols = text_cols[:, shard_rows:]
    text_rows = groups * own_text
    text_part = jnp.concatenate([dot(input_cols, wq_text), dot(gated_cols, wo_text)], axis=1)
    half = count // 2 * text_rows
    text_all = reduce_dp(text_part[half:].astype(bf16), text_part[:half], text_rows)

    tokens = jnp.concatenate(token_ring, axis=0)
    normal = layer_normal(tokens.astype(f32))
    image_input = ((1.0 + mods_i[1]) * normal + mods_i[0]).astype(bf16)
    proj_qk = dot(image_input, w_qk)
    proj_v = dot(image_input, w_v)
    att_image, att_text = attention_forward(proj_qk, proj_v, text_all, heads)

    mixed_part = dot(att_image, w_o, 1, 1).astype(bf16)
    mixed_blocks = [mixed_part[k * own_image : (k + 1) * own_image] for k in range(groups)]
    mixed_start, _ = lax.optimization_barrier((mixed_blocks[1 % groups], gated_ring[groups - 2]))
    travel = mixed_start
    for k in range(2, groups):
        travel = (context_shift(travel).astype(f32) + mixed_blocks[k].astype(f32)).astype(bf16)
    mixed_image = context_shift(travel).astype(f32) + mixed_blocks[0].astype(f32)

    back_blocks = [dot(gated, w_o).astype(bf16) for gated in gated_ring]
    back_q, back_k, back_v, back_text = attention_backward(
        proj_qk, proj_v, text_all, back_blocks, heads
    )
    gated_all = jnp.concatenate(gated_ring, axis=0)
    middle = width // 2
    go_odd = dot(gated_all[:, middle:], att_image, 0, 0).astype(bf16)
    go_even = dot(gated_all[:, :middle], att_image, 0, 0)
    grad_o_image = reduce_dp(go_odd, go_even, shard_rows)
    back_image = jnp.concatenate([back_q, back_k, back_v], axis=1)
    gq_odd = dot(image_input[:, middle:], back_image, 0, 0).astype(bf16)
    gq_even = dot(image_input[:, :middle], back_image, 0, 0)
    grad_q_image = reduce_dp(gq_odd, gq_even, shard_rows)
    spread = dot(jnp.concatenate([back_q, back_k], axis=1), w_qk, 1, 1) + dot(back_v, w_v, 1, 1)

    att_all = gather_small(att_text).reshape(count * text_rows, inner)
    back_flat = jnp.concatenate([back_text[0], back_text[1], back_text[2]], axis=1)
    back_all = gather_small(back_flat).reshape(count * text_rows, triple)
    grad_o_text = dot(gated_cols, att_all, 0, 0)
    grad_q_text = dot(input_cols, back_all, 0, 0)
    mixed_cols = dot(att_all, wo_text, 1, 1)
    spread_cols = dot(back_all, wq_text, 1, 1)
    ret = jnp.concatenate([mixed_cols, spread_cols], axis=1)
    ret = ret.reshape(count, groups, own_text, 2 * shard_rows)
    travel = ret[:, 1 % groups].astype(bf16)
    for k in range(2, groups):
        travel = (context_shift(travel).astype(f32) + ret[:, k]).astype(bf16)
    ret_own = (context_shift(travel).astype(f32) + ret[:, 0]).astype(bf16)
    ret_rows = jnp.stack(exchange([ret_own[p] for p in range(count)]), axis=1).astype(f32)
    mixed_text = ret_rows[:, :, :shard_rows].reshape(own_text, width)
    spread_text = ret_rows[:, :, shard_rows:].reshape(own_text, width)

    update_image = (mods_i[2] * mixed_image).astype(bf16)
    update_text = (mods_t[2] * mixed_text).astype(bf16)
    rel_slope_i, rel_slope_t, rel_normal_t = relative(
        me, image_slope[0].astype(f32), text_slope[0].astype(f32), text_normal
    )
    part_image = jnp.stack(
        [
            jnp.sum(spread, axis=0),
            jnp.sum(spread * normal, axis=0),
            jnp.sum(rel_slope_i * mixed_image, axis=0),
        ]
    )
    part_text = jnp.stack(
        [
            jnp.sum(spread_text, axis=0),
            jnp.sum(spread_text * rel_normal_t, axis=0),
            jnp.sum(rel_slope_t * mixed_text, axis=0),
        ]
    )
    sums = jnp.concatenate([part_image, part_text], axis=0)
    bit = 1
    while bit < groups:
        sums = sums + context_swap(sums, bit)
        bit *= 2
    out_image, out_text, modsum_image, modsum_text = leave(
        me, update_image, update_text, sums[:3], sums[3:]
    )
    return (
        out_image[None],
        out_text[None],
        grad_q_image.reshape(shard_rows, 3, heads, size),
        grad_q_text.reshape(shard_rows, 3, heads, size),
        grad_o_image.reshape(shard_rows, heads, size),
        grad_o_text.reshape(shard_rows, heads, size),
        modsum_image[None],
        modsum_text[None],
    )


def relative_kernel(me, a, b, c, a_o, b_o, c_o):
    a_o[...] = a[...]
    b_o[...] = b[...]
    c_o[...] = c[...]


def relative(me, *arrays):
    count = lax.axis_size("dp")
    width = arrays[0].shape[1] // count
    if width % 128:
        places = me ^ jnp.array(mask_order(), jnp.int32)
        return [take_blocks(a, places) for a in arrays]
    return pl.pallas_call(
        relative_kernel,
        grid_spec=pltpu.PrefetchScalarGridSpec(
            num_scalar_prefetch=1,
            grid=(count,),
            in_specs=[
                pl.BlockSpec((a.shape[0], width), lambda p, me: (0, relative_block(p, me, count)))
                for a in arrays
            ],
            out_specs=[pl.BlockSpec((a.shape[0], width), lambda p, me: (0, p)) for a in arrays],
        ),
        out_shape=[jax.ShapeDtypeStruct(a.shape, a.dtype) for a in arrays],
        name="relative",
    )(me, *arrays)


def solution(mesh):
    placed = (
        P("dp", "context", None),
        P("dp", "context", None),
        P("dp", None, None),
        P("dp", None, None),
        P("dp", None, "context", None),
        P("dp", None, "context", None),
        P("dp", "context", None),
        P("dp", "context", None),
        P("dp", "context", None),
        P("dp", "context", None),
    )
    return jax.shard_map(
        body,
        mesh=mesh,
        in_specs=placed,
        out_specs=(
            P("dp", "context", None),
            P("dp", "context", None),
            P("dp", None, "context", None),
            P("dp", None, "context", None),
            P("dp", "context", None),
            P("dp", "context", None),
            P("dp", None, None),
            P("dp", None, None),
        ),
        check_vma=False,
    )
```
